32 devices in a mesh: seq: 16 (over z, y, x), batch: 2 (over core).
Axes of the slice: x: 2, y: 2, z: 4, core: 2. Of those that a mesh axis runs over, the one named last changes fastest.
Arguments:
- hidden_in: bfloat16 [4, 2048, 1024], P('batch', 'seq'), may hold values from -6 to 6
- segment_ids: int32 [4, 2048], P('batch', 'seq'), may hold values from 0 to 7, never falling along the last dimension, each value on 1 to 1152 neighbouring positions
- query_weight: bfloat16 [1024, 1024], replicated, may hold values from -0.1875 to 0.1875
- key_weight: bfloat16 [1024, 1024], replicated, may hold values from -0.1875 to 0.1875
- value_weight: bfloat16 [1024, 1024], replicated, may hold values from -0.1875 to 0.1875
- out_weight: bfloat16 [1024, 1024], replicated, may hold values from -0.1875 to 0.1875
- up_weight: bfloat16 [1024, 4096], replicated, may hold values from -0.1875 to 0.1875
- gate_weight: bfloat16 [1024, 4096], replicated, may hold values from -0.1875 to 0.1875
- down_weight: bfloat16 [4096, 1024], replicated, may hold values from -0.09375 to 0.09375
- alpha_attend: float32 [1024], replicated, may hold values from 0.05 to 0.5
- alpha_feed: float32 [1024], replicated, may hold values from 0.05 to 0.5
- score_scale: float32 [1024], replicated, may hold values from 0.6 to 1.4
- up_scale: float32 [4096], replicated, may hold values from 0.5 to 2
- gate_scale: float32 [4096], replicated, may hold values from 0.5 to 2
- cotangent: bfloat16 [4, 2048, 1024], P('batch', 'seq'), may hold values from -6 to 6
Outputs:
- layer_out: bfloat16 [4, 2048, 1024], P('batch', 'seq')
- input_gradient: float32 [4, 2048, 1024], P('batch', 'seq')
- query_gradient: float32 [1024, 1024], P(('seq', 'batch'))
- key_gradient: float32 [1024, 1024], P(('seq', 'batch'))
- value_gradient: float32 [1024, 1024], P(('seq', 'batch'))
- out_gradient: float32 [1024, 1024], P(('seq', 'batch'))
- up_gradient: float32 [1024, 4096], P(('seq', 'batch'))
- gate_gradient: float32 [1024, 4096], P(('seq', 'batch'))
- down_gradient: float32 [4096, 1024], P(('seq', 'batch'))
- alpha_attend_gradient: float32 [1024], P(('seq', 'batch'))
- alpha_feed_gradient: float32 [1024], P(('seq', 'batch'))
- score_scale_gradient: float32 [1024], P(('seq', 'batch'))
- up_scale_gradient: float32 [4096], P(('seq', 'batch'))
- gate_scale_gradient: float32 [4096], P(('seq', 'batch'))
The draws below stay inside these ranges and needn't reach their ends.
Inputs may be any that keep to these rules, and one draw needn't show every extreme that they name: `segment_ids`: along each row the ids never fall, every id of 0 to 7 appears, and each id covers one run of 1 to 1152 positions.
All inputs are finite; a program needn't handle non-finite values.
Results may differ from the reference program's by a relative error of at most 0.015.
Values may be sent and summed in bfloat16 or wider, within the bound.
No kernel may reach another device: no remote copies, remote signals or barrier semaphores. Data moves between devices by JAX's collectives and lax.ppermute only.
A program may use at most 256 MiB of HBM per device.

```python
import math
from functools import partial
import jax
import jax.numpy as jnp
import numpy as np
from jax import lax

D = 1024
H = 16
HD = 64
FF = 4096
SEGS = 8
LENGTH = 2048
SEQS = 4
SEG_MOST = 1152


def strengthened(array, own_key, source, target, blocks, factor):
    owner, partner = [(jnp.arange(array.shape[axis_at]) // (array.shape[axis_at] // blocks)).reshape([-1 if axis == axis_at else 1 for axis in range(array.ndim)]) for axis_at in (source, target)]
    chosen = jax.random.permutation(own_key, blocks)[partner]
    strong = (owner == chosen) | (owner == (partner + blocks // 2) % blocks)
    return jnp.where(strong, factor * array, array)


def levels(rng, shape, cuts, low, high):
    loudness = 1.0
    for axis_at, blocks in cuts:
        heights = jax.random.uniform(jax.random.fold_in(jax.random.fold_in(rng, 6), axis_at), (blocks,), jnp.float32, low / len(cuts), high / len(cuts))
        loudness = loudness * jnp.repeat(jnp.exp(heights), shape[axis_at] // blocks).reshape((-1,) + (1,) * (len(shape) - 1 - axis_at))
    return loudness


def split_up(amount, total, limit, skew):
    loads = [(1 << 20) // math.isqrt(grade ** skew) + 1 for grade in range(2, amount + 1)]
    spare, holding = total - limit - (amount - 1), [1] * (amount - 1)
    while spare > 0:
        candidates = [i for i in range(amount - 1) if holding[i] < limit]
        whole, left = sum([loads[i] for i in candidates]), spare
        for i in candidates:
            extra = min(limit - holding[i], max(1, left * loads[i] // whole), spare)
            holding[i] = holding[i] + extra
            spare = spare - extra
    return np.array([limit] + holding)


def uneven(own_key, count, total, most, slope):
    if count == 2:
        one = jax.random.randint(own_key, (), max(1, total - most), min(most, total - 1) + 1)
        return jnp.stack([one, total - one])
    lengths = jnp.asarray(split_up(count, total, most, slope), jnp.int32)
    couples = (count - 1) // 2
    donor, sink = lengths[1:1 + 2 * couples:2], lengths[2:2 + 2 * couples:2]
    margin = jnp.minimum(donor - 1, most - sink)
    moved = jax.random.randint(jax.random.fold_in(own_key, 1), (couples,), 0, 1 << 20) % (margin + 1)
    lengths = lengths.at[1:1 + 2 * couples:2].set(donor - moved).at[2:2 + 2 * couples:2].set(sink + moved)
    return lengths[jax.random.permutation(jax.random.fold_in(own_key, 2), count)]


def gaussian(rng, extent, scale, reach, cuts=(), held_as=jnp.bfloat16):
    values = scale * jax.random.normal(rng, extent, jnp.float32)
    if cuts:
        values = values * levels(rng, extent, cuts, -0.22, 0.18)
    return jnp.clip(values, -reach, reach).astype(held_as)


def gaussian_with(own_key, dims, spread, most, shards, heavy, kind=jnp.bfloat16):
    drawn = spread * jax.random.normal(own_key, dims, jnp.float32)
    if shards:
        drawn = drawn * levels(own_key, dims, shards, -0.22, 0.18)
    return jnp.clip(strengthened(drawn, jax.random.fold_in(own_key, 3), *heavy), -most, most).astype(kind)


def setup_inputs(seed: int = 0) -> dict:
    arg_keys = jax.random.split(jax.random.key(seed), 16)
    return {
        "hidden_in": gaussian(arg_keys[0], (SEQS, LENGTH, D), 1.0, 6.0, ((0, 2), (1, 16))),
        "segment_ids": jax.vmap(lambda own: jnp.searchsorted(jnp.cumsum(uneven(own, SEGS, LENGTH, SEG_MOST, 2)), jnp.arange(LENGTH), side="right"))(jax.random.split(arg_keys[1], SEQS)).reshape((SEQS, LENGTH)).astype(jnp.int32),
        "query_weight": gaussian(arg_keys[2], (D, D), D ** -0.5, 0.1875),
        "key_weight": gaussian(arg_keys[3], (D, D), D ** -0.5, 0.1875),
        "value_weight": gaussian(arg_keys[4], (D, D), D ** -0.5, 0.1875),
        "out_weight": gaussian(arg_keys[5], (D, D), D ** -0.5, 0.1875),
        "up_weight": gaussian(arg_keys[6], (D, FF), D ** -0.5, 0.1875),
        "gate_weight": gaussian(arg_keys[7], (D, FF), D ** -0.5, 0.1875),
        "down_weight": gaussian(arg_keys[8], (FF, D), FF ** -0.5, 0.09375),
        "alpha_attend": jnp.clip(jnp.exp(jax.random.uniform(arg_keys[9], (D,), jnp.float32, math.log(0.05), math.log(0.5))), 0.05, 0.5),
        "alpha_feed": jnp.clip(jnp.exp(jax.random.uniform(arg_keys[10], (D,), jnp.float32, math.log(0.05), math.log(0.5))), 0.05, 0.5),
        "score_scale": jnp.clip(1.0 + 0.08 * jax.random.normal(arg_keys[11], (D,), jnp.float32), 0.6, 1.4),
        "up_scale": jnp.clip(jnp.exp(jax.random.uniform(arg_keys[12], (FF,), jnp.float32, math.log(0.5), math.log(2.0))), 0.5, 2.0),
        "gate_scale": jnp.clip(jnp.exp(jax.random.uniform(arg_keys[13], (FF,), jnp.float32, math.log(0.5), math.log(2.0))), 0.5, 2.0),
        "cotangent": gaussian_with(arg_keys[14], (SEQS, LENGTH, D), 1.0, 6.0, ((0, 2), (1, 16)), (1, 2, 16, 2.0)),
    }


@jax.custom_vjp
def low(v):
    return lax.optimization_barrier(v.astype(jnp.bfloat16)).astype(jnp.float32)

@jax.custom_vjp
def low_back(v):
    return v

def low_keep(v):
    return (low(v), None)

def low_pass(kept, grad):
    return (grad,)

def back_keep(v):
    return (v, None)

def back_low(kept, grad):
    return (low(grad),)
low.defvjp(low_keep, low_pass)
low_back.defvjp(back_keep, back_low)
highest = lax.Precision.HIGHEST

def matmul(left, right):
    return jnp.dot(left, right, precision=highest, preferred_element_type=jnp.float32)

def normed(values):
    return values * lax.rsqrt(lax.optimization_barrier(jnp.mean(values * values, axis=-1, keepdims=True)) + 1e-06)

def blend(hidden, branch, alpha):
    return normed(hidden + alpha * (normed(branch) - hidden))

def rotate(values, cosine, sine):
    half = values.shape[-1] // 2
    first = values[..., :half]
    second = values[..., half:]
    return jnp.concatenate([first * cosine - second * sine, second * cosine + first * sine], axis=-1)

def head_unit(values, scale):
    shaped = scale.reshape(values.shape[-2], values.shape[-1])
    return values * lax.rsqrt(lax.optimization_barrier(jnp.sum(values * values, axis=-1, keepdims=True)) + 1e-06) * shaped

def frequencies():
    half = HD // 2
    return 1.0 / 10000.0 ** (jnp.arange(half, dtype=jnp.float32) / half)

def positions(row_ids):
    places = jnp.arange(row_ids.shape[0], dtype=jnp.int32)
    match = row_ids[:, None] == jnp.arange(SEGS, dtype=jnp.int32)[None, :]
    starts = lax.optimization_barrier(jnp.min(jnp.where(match, places[:, None], row_ids.shape[0]), axis=0))
    begin = lax.optimization_barrier(jnp.sum(jnp.where(match, starts[None, :], 0), axis=1))
    return places - begin

def attention(queries, keys, values, row_ids):
    length = queries.shape[0]
    width = math.gcd(length, 512)
    places = jnp.arange(length, dtype=jnp.int32)

    def block(parts):
        query_block, id_block, place_block = parts
        scores = low_back(math.sqrt(HD) * jnp.einsum('qhd,khd->hqk', query_block, keys, precision=highest))
        allowed = (id_block[:, None] == row_ids[None, :]) & (places[None, :] <= place_block[:, None])
        expo = jnp.where(allowed[None], jnp.exp(scores), 0.0)
        totals = low_back(lax.optimization_barrier(jnp.sum(expo, axis=-1)))
        summed = low_back(jnp.einsum('hqk,khd->qhd', low(expo), values, precision=highest))
        return summed / jnp.transpose(totals)[:, :, None]
    shaped = (queries.reshape(length // width, width, H, HD), row_ids.reshape(length // width, width), places.reshape(length // width, width))
    return lax.map(jax.checkpoint(block), shaped).reshape(length, H * HD)

def layer(hidden_in, query_weight, key_weight, value_weight, out_weight, up_weight, gate_weight, down_weight, alpha_attend, alpha_feed, score_scale, up_scale, gate_scale, cosine, sine, row_ids):
    length = hidden_in.shape[0]
    low_in = low(hidden_in)
    query_raw = low_back(matmul(low_in, query_weight)).reshape(length, H, HD)
    key_raw = low_back(matmul(low_in, key_weight)).reshape(length, H, HD)
    value_low = low_back(low(matmul(low_in, value_weight))).reshape(length, H, HD)
    queries = low(head_unit(rotate(query_raw, cosine, sine), score_scale))
    keys = low(head_unit(rotate(key_raw, cosine, sine), score_scale))
    mixed = low(attention(queries, keys, value_low, row_ids))
    attended = low_back(matmul(mixed, out_weight))
    middle = blend(hidden_in, attended, alpha_attend)
    middle_low = low(middle)
    up_part = low_back(matmul(middle_low, up_weight))
    gate_part = low_back(matmul(middle_low, gate_weight))
    inner = low(up_part * up_scale * jax.nn.silu(gate_part * gate_scale))
    branch = low_back(matmul(inner, down_weight))
    return blend(middle, branch, alpha_feed)

def reference(hidden_in, segment_ids, query_weight, key_weight, value_weight, out_weight, up_weight, gate_weight, down_weight, alpha_attend, alpha_feed, score_scale, up_scale, gate_scale, cotangent):
    params = tuple((matrix.astype(jnp.float32) for matrix in (query_weight, key_weight, value_weight, out_weight, up_weight, gate_weight, down_weight, alpha_attend, alpha_feed, score_scale, up_scale, gate_scale)))
    freqs = frequencies()

    def per_row(totals, row):
        row_in, row_ids, row_cot = row
        angles = positions(row_ids).astype(jnp.float32)[:, None] * freqs[None, :]
        cosine = jnp.cos(angles)[:, None, :]
        sine = jnp.sin(angles)[:, None, :]
        bound = partial(layer, cosine=cosine, sine=sine, row_ids=row_ids)
        result, backward = jax.vjp(bound, row_in.astype(jnp.float32), *params)
        grads = backward(row_cot.astype(jnp.float32))
        totals = tuple((before + update for before, update in zip(totals, grads[1:])))
        return (totals, (result.astype(jnp.bfloat16), grads[0]))
    start = tuple((jnp.zeros_like(member) for member in params))
    totals, (outputs, input_grads) = lax.scan(per_row, start, (hidden_in, segment_ids, cotangent))
    return (outputs, input_grads, totals[0], totals[1], totals[2], totals[3], totals[4], totals[5], totals[6], totals[7], totals[8], totals[9], totals[10], totals[11])
```

```python
import math

import jax
import jax.numpy as jnp
from jax import lax
from jax.experimental import pallas as pl
from jax.experimental.pallas import tpu as pltpu
from jax.sharding import PartitionSpec as P

H = 16
HD = 64
SEGS = 8
LANES = 128
BF = jnp.bfloat16
F32 = jnp.float32


def normed(values):
    return values * lax.rsqrt(jnp.mean(values * values, axis=-1, keepdims=True) + 1e-06)


def blend(hidden, branch, alpha):
    return normed(hidden + alpha * (normed(branch) - hidden))


def gated(up_part, gate_part, up_scale, gate_scale):
    return up_part * up_scale * jax.nn.silu(gate_part * gate_scale)


def matmul(left, right):
    return jnp.dot(left, right, preferred_element_type=F32)


def right_trans(left, right):
    return lax.dot_general(left, right, (((1,), (1,)), ((), ())), preferred_element_type=F32)


def left_trans(left, right):
    return lax.dot_general(left, right, (((0,), (0,)), ((), ())), preferred_element_type=F32)


def split_dot(values, ones):
    high = values.astype(BF)
    low = (values - high.astype(F32)).astype(BF)
    return matmul(high, ones) + matmul(low, ones)


def lane_ids(rows):
    return lax.broadcasted_iota(jnp.int32, (rows, LANES), 1)


def head_blocks():
    one = lax.broadcasted_iota(jnp.int32, (LANES, LANES), 0) // HD
    two = lax.broadcasted_iota(jnp.int32, (LANES, LANES), 1) // HD
    return jnp.where(one == two, 1.0, 0.0).astype(BF)


def swapped_halves(values, lanes):
    half = HD // 2
    ahead = pltpu.roll(values, LANES - half, 1)
    behind = pltpu.roll(values, half, 1)
    return jnp.where(lanes % HD < half, ahead, behind)


def frequencies():
    half = HD // 2
    return 1.0 / 10000.0 ** (jnp.arange(half, dtype=F32) / half)


def rope_tables(places):
    angles = places.astype(F32)[:, None] * frequencies()[None, :]
    cosine = jnp.cos(angles)
    sine = jnp.sin(angles)
    return (
        jnp.concatenate([cosine, cosine] * (LANES // HD), axis=1),
        jnp.concatenate([-sine, sine] * (LANES // HD), axis=1),
    )


def project_kernel(x_ref, wq_ref, wk_ref, wv_ref, cos_ref, sin_ref, scale_ref, q0_ref, k0_ref, unit_ref):
    rows, per, _, length, width = unit_ref.shape
    block = wq_ref.shape[1]
    x = x_ref[...]
    q0 = matmul(x, wq_ref[...])
    k0 = matmul(x, wk_ref[...])
    v = matmul(x, wv_ref[...]).astype(BF)
    q0_ref[...] = q0
    k0_ref[...] = k0
    lanes = lane_ids(length)
    ones = head_blocks()
    per_tile = LANES // width
    for row in range(rows):
        for tile in range(block // LANES):
            there = (slice(row * length, (row + 1) * length), slice(tile * LANES, (tile + 1) * LANES))
            scale = scale_ref[:, tile * LANES : (tile + 1) * LANES]
            cosine = cos_ref[there[0], :]
            sine = sin_ref[there[0], :]
            results = []
            for raw in (q0, k0):
                z = raw[there]
                rot = z * cosine + swapped_halves(z, lanes) * sine
                total = split_dot(z * z, ones)
                results.append((rot * lax.rsqrt(total + 1e-06) * scale).astype(BF))
            results.append(v[there])
            for part in range(per_tile):
                for kind in range(3):
                    unit_ref[row, tile * per_tile + part, kind] = results[kind][
                        :, part * width : (part + 1) * width
                    ]


def project(x, wq, wk, wv, cosine, sine, scale, rows, width):
    tokens, model = x.shape
    length = tokens // rows
    block = 256
    per = block // width
    return pl.pallas_call(
        project_kernel,
        grid=(model // block,),
        in_specs=[
            pl.BlockSpec((tokens, model), lambda j: (0, 0)),
            pl.BlockSpec((model, block), lambda j: (0, j)),
            pl.BlockSpec((model, block), lambda j: (0, j)),
            pl.BlockSpec((model, block), lambda j: (0, j)),
            pl.BlockSpec((tokens, LANES), lambda j: (0, 0)),
            pl.BlockSpec((tokens, LANES), lambda j: (0, 0)),
            pl.BlockSpec((1, block), lambda j: (0, j)),
        ],
        out_specs=[
            pl.BlockSpec((tokens, block), lambda j: (0, j)),
            pl.BlockSpec((tokens, block), lambda j: (0, j)),
            pl.BlockSpec((rows, per, 3, length, width), lambda j: (0, j, 0, 0, 0)),
        ],
        out_shape=[
            jax.ShapeDtypeStruct((tokens, model), F32),
            jax.ShapeDtypeStruct((tokens, model), F32),
            jax.ShapeDtypeStruct((rows, model // width, 3, length, width), BF),
        ],
        name="project",
    )(x, wq, wk, wv, cosine, sine, scale)


def unproject_kernel(grad_ref, q0_ref, k0_ref, cos_ref, sin_ref, scale_ref, gq_ref, gk_ref, gv_ref, gs_ref):
    rows, per, _, length, width = grad_ref.shape
    block = q0_ref.shape[1]
    lanes = lane_ids(length)
    ones = head_blocks()
    per_tile = LANES // width
    for tile in range(block // LANES):
        across = slice(tile * LANES, (tile + 1) * LANES)
        scale = scale_ref[:, across]
        slope = jnp.zeros((1, LANES), F32)
        for row in range(rows):
            there = (slice(row * length, (row + 1) * length), across)
            cosine = cos_ref[there[0], :]
            sine = sin_ref[there[0], :]
            parts = []
            for kind in range(3):
                pieces = [grad_ref[row, tile * per_tile + part, kind] for part in range(per_tile)]
                parts.append(pieces[0] if per_tile == 1 else jnp.concatenate(pieces, axis=1))
            for raw_ref, grad, out_ref in ((q0_ref, parts[0], gq_ref), (k0_ref, parts[1], gk_ref)):
                z = raw_ref[there]
                g = grad.astype(F32)
                rot = z * cosine + swapped_halves(z, lanes) * sine
                inverse = lax.rsqrt(split_dot(z * z, ones) + 1e-06)
                unit = rot * inverse
                slope = slope + jnp.sum(g * unit, axis=0, keepdims=True)
                g = g * scale
                g = inverse * (g - unit * split_dot(g * unit, ones))
                g = g * cosine - swapped_halves(g, lanes) * sine
                out_ref[there] = g.astype(BF)
            gv_ref[there] = parts[2]
        gs_ref[:, across] = slope


def unproject(grad, q0, k0, cosine, sine, scale):
    rows, heads, _, length, width = grad.shape
    tokens, model = q0.shape
    block = 256
    per = block // width
    wide = pl.BlockSpec((tokens, block), lambda j: (0, j))
    table = pl.BlockSpec((tokens, LANES), lambda j: (0, 0))
    line = pl.BlockSpec((1, block), lambda j: (0, j))
    return pl.pallas_call(
        unproject_kernel,
        grid=(model // block,),
        in_specs=[
            pl.BlockSpec((rows, per, 3, length, width), lambda j: (0, j, 0, 0, 0)),
            wide,
            wide,
            table,
            table,
            line,
        ],
        out_specs=[wide, wide, wide, line],
        out_shape=[
            jax.ShapeDtypeStruct((tokens, model), BF),
            jax.ShapeDtypeStruct((tokens, model), BF),
            jax.ShapeDtypeStruct((tokens, model), BF),
            jax.ShapeDtypeStruct((1, model), F32),
        ],
        name="unproject",
    )(grad, q0, k0, cosine, sine, scale)


def widened(values):
    rows, width = values.shape
    if width == LANES:
        return values
    return jnp.concatenate([values, jnp.zeros((rows, LANES - width), values.dtype)], axis=1)


def in_head(rows, head):
    return lane_ids(rows) // HD == head


def attend_kernel(low_ref, begin_ref, unit_ref, o_ref, inv_ref, qs, ks, vs, acc):
    sources, _, _, length, width = unit_ref.shape
    heads = width // HD
    block = acc.shape[1]
    count = sources * length // block
    unit = pl.program_id(0)
    chunk = block // length

    def prepare(source, carry):
        at = pl.ds(pl.multiple_of(source * length, length), length)
        q = widened(unit_ref[source, 0, 0]) * jnp.asarray(math.sqrt(HD), BF)
        v = widened(unit_ref[source, 0, 2])
        ks[at, :] = widened(unit_ref[source, 0, 1])
        for head in range(heads):
            own = in_head(length, head)
            qs[head, at, :] = jnp.where(own, q, jnp.zeros_like(q))
            vs[head, at, :] = jnp.where(own, v, jnp.ones_like(v))
        return carry

    lax.fori_loop(0, sources, prepare, 0)

    def query_turn(turn, carry):
        first = pl.multiple_of(turn * block, block)
        begin = jnp.broadcast_to(begin_ref[0, :, pl.ds(first, block)], (LANES, block))
        begin = jnp.transpose(begin)[:, :1]
        places = first + lax.broadcasted_iota(jnp.int32, (block, 1), 0)
        acc[...] = jnp.zeros_like(acc)

        def key_turn(other, inner):
            start = pl.multiple_of(other * block, block)
            keys = ks[pl.ds(start, block), :]
            across = start + lax.broadcasted_iota(jnp.int32, (1, block), 1)
            allowed = (across.astype(F32) >= begin) & (across <= places)
            for head in range(heads):
                scores = right_trans(qs[head, pl.ds(first, block), :], keys)
                expo = jnp.where(allowed, jnp.exp(scores), 0.0)
                acc[head] += matmul(expo.astype(BF), vs[head, pl.ds(start, block), :])
            return inner

        lax.fori_loop(low_ref[unit, turn], turn + 1, key_turn, 0)
        output = None
        inverse = None
        for head in range(heads):
            summed = acc[head]
            one = 1.0 / pltpu.roll(summed, HD, 1)
            two = summed * one
            if output is None:
                output, inverse = two, one
            else:
                own = in_head(block, head)
                output = jnp.where(own, two, output)
                inverse = jnp.where(own, one, inverse)
        for part in range(chunk):
            source = turn * chunk + part
            rows = slice(part * length, (part + 1) * length)
            o_ref[source, 0] = output[rows, :width].astype(BF)
            inv_ref[source, 0] = inverse[rows]
        return carry

    lax.fori_loop(0, count, query_turn, 0)


def attend(low, begin, unit, block):
    sources, units, _, length, width = unit.shape
    total = sources * length
    heads = width // HD
    return pl.pallas_call(
        attend_kernel,
        grid_spec=pltpu.PrefetchScalarGridSpec(
            num_scalar_prefetch=1,
            grid=(units,),
            in_specs=[
                pl.BlockSpec((1, 1, total), lambda u, low: (u, 0, 0)),
                pl.BlockSpec((sources, 1, 3, length, width), lambda u, low: (0, u, 0, 0, 0)),
            ],
            out_specs=[
                pl.BlockSpec((sources, 1, length, width), lambda u, low: (0, u, 0, 0)),
                pl.BlockSpec((sources, 1, length, LANES), lambda u, low: (0, u, 0, 0)),
            ],
            scratch_shapes=[
                pltpu.VMEM((heads, total, LANES), BF),
                pltpu.VMEM((total, LANES), BF),
                pltpu.VMEM((heads, total, LANES), BF),
                pltpu.VMEM((heads, block, LANES), F32),
            ],
        ),
        out_shape=[
            jax.ShapeDtypeStruct((sources, units, length, width), BF),
            jax.ShapeDtypeStruct((sources, units, length, LANES), F32),
        ],
        name="attend",
    )(low, begin, unit)


def attend_back_kernel(
    high_ref, begin_ref, unit_ref, go_ref, o_ref, inv_ref, grad_ref, qs, k8, ks, vs, da, dam, dq, dk, dv
):
    sources, _, _, length, width = unit_ref.shape
    heads = width // HD
    block = dk.shape[0]
    count = sources * length // block
    unit = pl.program_id(0)
    chunk = block // length
    root = jnp.asarray(math.sqrt(HD), BF)

    def prepare(source, carry):
        at = pl.ds(pl.multiple_of(source * length, length), length)
        q = widened(unit_ref[source, 0, 0]) * root
        k = widened(unit_ref[source, 0, 1])
        v = widened(unit_ref[source, 0, 2])
        ks[at, :] = k
        k = k * root
        go = widened(go_ref[source, 0]).astype(F32) * inv_ref[source, 0]
        product = go * widened(o_ref[source, 0]).astype(F32)
        for head in range(heads):
            own = in_head(length, head)
            qs[head, at, :] = jnp.where(own, q, jnp.zeros_like(q))
            k8[head, at, :] = jnp.where(own, k, jnp.zeros_like(k))
            vs[head, at, :] = jnp.where(own, v, jnp.ones_like(v))
            mine = jnp.where(own, go, 0.0)
            dam[head, at, :] = mine.astype(BF)
            slope = -jnp.sum(jnp.where(own, product, 0.0), axis=1, keepdims=True)
            spare = lane_ids(length) == ((head + 1) * HD) % LANES
            da[head, at, :] = jnp.where(spare, slope, mine).astype(BF)
        dq[at, :] = jnp.zeros((length, LANES), F32)
        return carry

    lax.fori_loop(0, sources, prepare, 0)

    def key_turn(turn, carry):
        start = pl.multiple_of(turn * block, block)
        keys = ks[pl.ds(start, block), :]
        along = start + lax.broadcasted_iota(jnp.int32, (block, 1), 0)
        dk[...] = jnp.zeros_like(dk)
        dv[...] = jnp.zeros_like(dv)

        def query_turn(other, inner):
            first = pl.multiple_of(other * block, block)
            begin = begin_ref[0, :, pl.ds(first, block)]
            across = first + lax.broadcasted_iota(jnp.int32, (1, block), 1)
            allowed = (along.astype(F32) >= begin) & (along <= across)
            for head in range(heads):
                queries = qs[head, pl.ds(first, block), :]
                scores = right_trans(keys, queries)
                expo = jnp.where(allowed, jnp.exp(scores), 0.0)
                slopes = right_trans(vs[head, pl.ds(start, block), :], da[head, pl.ds(first, block), :])
                slopes = (expo * slopes).astype(BF)
                dk[...] += matmul(slopes, queries)
                dv[...] += matmul(expo.astype(BF), dam[head, pl.ds(first, block), :])
                dq[pl.ds(first, block), :] += left_trans(slopes, k8[head, pl.ds(start, block), :])
            return inner

        lax.fori_loop(turn, high_ref[unit, turn] + 1, query_turn, 0)
        for part in range(chunk):
            source = turn * chunk + part
            rows = slice(part * length, (part + 1) * length)
            grad_ref[source, 0, 1] = dk[rows, :width].astype(BF)
            grad_ref[source, 0, 2] = dv[rows, :width].astype(BF)
        return carry

    lax.fori_loop(0, count, key_turn, 0)

    def finish(source, carry):
        at = pl.ds(pl.multiple_of(source * length, length), length)
        grad_ref[source, 0, 0] = dq[at, :width].astype(BF)
        return carry

    lax.fori_loop(0, sources, finish, 0)


def attend_back(high, begin, unit, go, o, inverse, block):
    sources, units, _, length, width = unit.shape
    total = sources * length
    heads = width // HD
    flat = pl.BlockSpec((sources, 1, length, width), lambda u, high: (0, u, 0, 0))
    triple = pl.BlockSpec((sources, 1, 3, length, width), lambda u, high: (0, u, 0, 0, 0))
    return pl.pallas_call(
        attend_back_kernel,
        grid_spec=pltpu.PrefetchScalarGridSpec(
            num_scalar_prefetch=1,
            grid=(units,),
            in_specs=[
                pl.BlockSpec((1, 1, total), lambda u, high: (u, 0, 0)),
                triple,
                flat,
                flat,
                pl.BlockSpec((sources, 1, length, LANES), lambda u, high: (0, u, 0, 0)),
            ],
            out_specs=[triple],
            scratch_shapes=[
                pltpu.VMEM((heads, total, LANES), BF),
                pltpu.VMEM((heads, total, LANES), BF),
                pltpu.VMEM((total, LANES), BF),
                pltpu.VMEM((heads, total, LANES), BF),
                pltpu.VMEM((heads, total, LANES), BF),
                pltpu.VMEM((heads, total, LANES), BF),
                pltpu.VMEM((total, LANES), F32),
                pltpu.VMEM((block, LANES), F32),
                pltpu.VMEM((block, LANES), F32),
            ],
        ),
        out_shape=[jax.ShapeDtypeStruct((sources, units, 3, length, width), BF)],
        name="attend_back",
    )(high, begin, unit, go, o, inverse)[0]


def position_of(relative, order):
    bits = len(order)
    return sum(((relative >> bit) & 1) << (bits - 1 - place) for place, bit in enumerate(order))


def weight_kernel(where_ref, own_left, pair_left, own_right, pair_right, send_ref, keep_ref, acc, *, order):
    half, height, _ = send_ref.shape
    acc[...] = left_trans(own_left[...], own_right[...]) + left_trans(pair_left[...], pair_right[...])
    me = where_ref[0]
    for relative in range(2 * half):
        place = position_of(relative, order)
        source = pl.multiple_of((me ^ relative) * height, height)
        block = acc[pl.ds(source, height), :].astype(BF)
        if place >= half:
            send_ref[place - half] = block
        else:
            keep_ref[place] = block


def weight_terms(place, own_left, pair_left, own_right, pair_right, column, columns, order):
    tokens, deep = own_left.shape
    half_width = pair_right.shape[1]
    count = 1 << len(order)
    height = deep // count
    tile = min(256, columns)
    shift = column // tile
    core_shift = half_width // tile
    body = lambda *refs: weight_kernel(*refs, order=order)
    shape = jax.ShapeDtypeStruct((count // 2, height, columns), BF)
    out = pl.BlockSpec((count // 2, height, tile), lambda j, where: (0, 0, j))
    return pl.pallas_call(
        body,
        grid_spec=pltpu.PrefetchScalarGridSpec(
            num_scalar_prefetch=1,
            grid=(columns // tile,),
            in_specs=[
                pl.BlockSpec((tokens, deep), lambda j, where: (0, 0)),
                pl.BlockSpec((tokens, deep), lambda j, where: (0, 0)),
                pl.BlockSpec((tokens, tile), lambda j, where: (0, where[1] * core_shift + shift + j)),
                pl.BlockSpec((tokens, tile), lambda j, where: (0, shift + j)),
            ],
            out_specs=[out, out],
            scratch_shapes=[pltpu.VMEM((deep, tile), F32)],
        ),
        out_shape=[shape, shape],
        name="weight_terms",
    )(place, own_left, pair_left, own_right, pair_right)


def scattered(send, keep, order):
    count = 1 << len(order)
    got = []
    moving = send
    for step, bit in enumerate(order):
        got.append(lax.ppermute(moving, "seq", [(i, i ^ (1 << bit)) for i in range(count)]))
        size = count >> (step + 2)
        if step + 1 < len(order):
            moving = keep[size : 2 * size].astype(F32)
            for piece in got:
                moving = moving + piece[size : 2 * size].astype(F32)
            moving = moving.astype(BF)
    total = keep[0].astype(F32)
    for piece in got:
        total = total + piece[0].astype(F32)
    return total


def paired(values):
    count = lax.axis_size("batch")
    return lax.ppermute(values, "batch", [(i, i ^ 1) for i in range(count)])


def batch_finished(values):
    count = lax.axis_size("batch")
    mine = lax.axis_index("batch")
    height, half_width = values.shape
    values = values.reshape(count, height // count, half_width)
    bit = count.bit_length() - 2
    while bit > 0:
        values = values.reshape((2, values.shape[0] // 2) + values.shape[1:])
        side = (mine >> bit) & 1
        sent = lax.dynamic_index_in_dim(values, 1 - side, 0, keepdims=False)
        kept = lax.dynamic_index_in_dim(values, side, 0, keepdims=False)
        pairs = [(i, i ^ (1 << bit)) for i in range(count)]
        values = kept + lax.ppermute(sent, "batch", pairs)
        bit -= 1
    side = mine & 1
    sent = lax.dynamic_index_in_dim(values, 1 - side, 0, keepdims=False)
    kept = lax.dynamic_index_in_dim(values, side, 0, keepdims=False)
    taken = paired(sent)
    first = jnp.where(side == 0, kept, taken)
    second = jnp.where(side == 0, taken, kept)
    return jnp.concatenate([first, second], axis=1)


def other_half(values):
    side = lax.axis_index("batch") & 1
    half = values.shape[1] // 2
    return paired(lax.dynamic_slice_in_dim(values, (1 - side) * half, half, 1))


def weight_gradient(place, left, pair_left, right, pieces):
    pair_right = other_half(right)
    half = pair_right.shape[1]
    column = 0
    results = []
    for share, order in pieces:
        columns = half // share
        send, keep = weight_terms(place, left, pair_left, right, pair_right, column, columns, order)
        results.append(scattered(send, keep, order))
        column += columns
    whole = results[0] if len(results) == 1 else jnp.concatenate(results, axis=1)
    return batch_finished(whole)


def body(
    hidden_in,
    segment_ids,
    query_weight,
    key_weight,
    value_weight,
    out_weight,
    up_weight,
    gate_weight,
    down_weight,
    alpha_attend,
    alpha_feed,
    score_scale,
    up_scale,
    gate_scale,
    cotangent,
):
    rows, length, width = hidden_in.shape
    tokens = rows * length
    seqs = lax.axis_size("seq")
    batches = lax.axis_size("batch")
    me = lax.axis_index("seq")
    place = jnp.stack([me, lax.axis_index("batch") & 1]).astype(jnp.int32)
    total = seqs * length
    pack = LANES // HD
    if (H // pack * rows) % seqs:
        pack = 1
    span = pack * HD
    groups = H // pack
    units = groups * rows // seqs
    block = math.gcd(256, total)
    bits = seqs.bit_length() - 1
    order_a = tuple(range(bits))
    order_b = (1, 0) + order_a[2:]

    def exchanged(values):
        return lax.all_to_all(values, "seq", 0, 0, tiled=True)

    ids = exchanged(jnp.broadcast_to(segment_ids[None], (seqs, rows, length)))
    ids = jnp.transpose(ids.reshape(seqs, rows, length), (1, 0, 2)).reshape(rows, total)
    labels = jnp.arange(SEGS, dtype=jnp.int32)
    starts = jnp.sum(ids[:, None, :] < labels[None, :, None], axis=2)
    places = me * length + jnp.arange(length, dtype=jnp.int32)
    match = segment_ids[:, None, :] == labels[None, :, None]
    offsets = places[None, :] - jnp.sum(jnp.where(match, starts[:, :, None], 0), axis=1)
    cosine, sine = rope_tables(offsets.reshape(tokens))
    unit_rows = (me * units + jnp.arange(units, dtype=jnp.int32)) // groups
    ids = jnp.take(ids, unit_rows, axis=0)
    starts = jnp.sum(ids[:, None, :] < labels[None, :, None], axis=2)
    ends = jnp.sum(ids[:, None, :] <= labels[None, :, None], axis=2)
    match = ids[:, None, :] == labels[None, :, None]
    begin = jnp.sum(jnp.where(match, starts[:, :, None], 0), axis=1)
    end = jnp.sum(jnp.where(match, ends[:, :, None], 0), axis=1)
    low = (begin[:, ::block] // block).astype(jnp.int32)
    high = ((end[:, block - 1 :: block] - 1) // block).astype(jnp.int32)
    begin = begin.astype(F32).reshape(units, 1, total)

    flat_in = hidden_in.reshape(tokens, width)
    pair_in = paired(flat_in)
    hidden = flat_in.astype(F32)
    scale_row = score_scale.reshape(1, width)

    query_raw, key_raw, sent = project(
        flat_in, query_weight, key_weight, value_weight, cosine, sine, scale_row, rows, span
    )
    unit = exchanged(sent.reshape(rows * groups, 3, length, span)).reshape(seqs, units, 3, length, span)
    out_unit, inverse = attend(low, begin, unit, block)
    mixed = exchanged(out_unit.reshape(seqs * units, length, span)).reshape(rows, groups, length, span)
    mixed = jnp.transpose(mixed, (0, 2, 1, 3)).reshape(tokens, width)
    pair_mixed = paired(mixed)

    attended = matmul(mixed, out_weight)
    middle, first_back = jax.vjp(blend, hidden, attended, alpha_attend)
    middle_low = middle.astype(BF)
    pair_middle = paired(middle_low)
    up_part = matmul(middle_low, up_weight)
    gate_part = matmul(middle_low, gate_weight)
    inner_act, gate_back = jax.vjp(gated, up_part, gate_part, up_scale, gate_scale)
    inner_low = inner_act.astype(BF)
    pair_inner = paired(inner_low)
    branch = matmul(inner_low, down_weight)
    result, second_back = jax.vjp(blend, middle, branch, alpha_feed)
    layer_out = result.astype(BF).reshape(rows, length, width)
    middle_grad, branch_grad, alpha_feed_grad = second_back(cotangent.reshape(tokens, width).astype(F32))
    branch_low = branch_grad.astype(BF)
    inner_grad = right_trans(branch_low, down_weight)
    up_grad, gate_grad, up_scale_grad, gate_scale_grad = gate_back(inner_grad)
    up_low = up_grad.astype(BF)
    gate_low = gate_grad.astype(BF)
    middle_grad = middle_grad + right_trans(up_low, up_weight) + right_trans(gate_low, gate_weight)
    hidden_grad, attended_grad, alpha_attend_grad = first_back(middle_grad)
    attended_low = attended_grad.astype(BF)
    mixed_grad = right_trans(attended_low, out_weight).astype(BF)
    mixed_grad = jnp.transpose(mixed_grad.reshape(rows, length, groups, span), (0, 2, 1, 3))
    go_unit = exchanged(mixed_grad.reshape(rows * groups, length, span)).reshape(seqs, units, length, span)

    down_gradient = weight_gradient(
        place, inner_low, pair_inner, branch_low, ((2, order_a), (2, order_b))
    )
    up_gradient = weight_gradient(place, middle_low, pair_middle, up_low, ((1, order_a),))
    gate_gradient = weight_gradient(place, middle_low, pair_middle, gate_low, ((1, order_b),))
    out_gradient = weight_gradient(
        place, mixed, pair_mixed, attended_low, ((2, order_a), (2, order_b))
    )

    grad_unit = attend_back(high, begin, unit, go_unit, out_unit, inverse, block)
    grads = exchanged(grad_unit.reshape(seqs * units, 3, length, span)).reshape(rows, groups, 3, length, span)
    query_low, key_low, value_low, score_grad = unproject(grads, query_raw, key_raw, cosine, sine, scale_row)
    input_grad = (
        hidden_grad
        + right_trans(query_low, query_weight)
        + right_trans(key_low, key_weight)
        + right_trans(value_low, value_weight)
    )
    query_gradient = weight_gradient(place, flat_in, pair_in, query_low, ((1, order_a),))
    key_gradient = weight_gradient(place, flat_in, pair_in, key_low, ((1, order_b),))
    value_gradient = weight_gradient(place, flat_in, pair_in, value_low, ((2, order_a), (2, order_b)))

    def summed(parts):
        devices = seqs * batches
        cuts = [part.reshape(devices, part.size // devices) for part in parts]
        mine = lax.all_to_all(jnp.concatenate(cuts, axis=1), ("seq", "batch"), 0, 0, tiled=True)
        mine = jnp.sum(mine, axis=0)
        outs = []
        at = 0
        for cut in cuts:
            outs.append(mine[at : at + cut.shape[1]])
            at += cut.shape[1]
        return outs

    small = summed((alpha_attend_grad, alpha_feed_grad, up_scale_grad, gate_scale_grad))
    (score_scale_gradient,) = summed((score_grad,))
    return (
        layer_out,
        input_grad.reshape(rows, length, width),
        query_gradient,
        key_gradient,
        value_gradient,
        out_gradient,
        up_gradient,
        gate_gradient,
        down_gradient,
        small[0],
        small[1],
        score_scale_gradient,
        small[2],
        small[3],
    )


def solution(mesh):
    wide = P("batch", "seq", None)
    in_specs = (wide, P("batch", "seq")) + (P(),) * 12 + (wide,)
    split = P(("seq", "batch"), None)
    out_specs = (wide, wide) + (split,) * 7 + (P(("seq", "batch")),) * 5
    return jax.shard_map(body, mesh=mesh, in_specs=in_specs, out_specs=out_specs, check_vma=False)
```

```python
import math

import jax
import jax.numpy as jnp
from jax import lax
from jax.experimental import pallas as pl
from jax.experimental.pallas import tpu as pltpu
from jax.sharding import PartitionSpec as P

H = 16
HD = 64
SEGS = 8
LANES = 128
BF = jnp.bfloat16
F32 = jnp.float32


def matmul(left, right):
    return jnp.dot(left, right, preferred_element_type=F32)


def right_trans(left, right):
    return lax.dot_general(left, right, (((1,), (1,)), ((), ())), preferred_element_type=F32)


def left_trans(left, right):
    return lax.dot_general(left, right, (((0,), (0,)), ((), ())), preferred_element_type=F32)


def split_dot(values, ones):
    high = values.astype(BF)
    low = (values - high.astype(F32)).astype(BF)
    return matmul(high, ones) + matmul(low, ones)


def lane_ids(rows):
    return lax.broadcasted_iota(jnp.int32, (rows, LANES), 1)


def head_blocks():
    one = lax.broadcasted_iota(jnp.int32, (LANES, LANES), 0) // HD
    two = lax.broadcasted_iota(jnp.int32, (LANES, LANES), 1) // HD
    return jnp.where(one == two, 1.0, 0.0).astype(BF)


def swapped_halves(values, lanes):
    half = HD // 2
    ahead = pltpu.roll(values, LANES - half, 1)
    behind = pltpu.roll(values, half, 1)
    return jnp.where(lanes % HD < half, ahead, behind)


def frequencies():
    half = HD // 2
    return 1.0 / 10000.0 ** (jnp.arange(half, dtype=F32) / half)


def rope_tables(places):
    angles = places.astype(F32)[:, None] * frequencies()[None, :]
    cosine = jnp.cos(angles)
    sine = jnp.sin(angles)
    return (
        jnp.concatenate([cosine, cosine] * (LANES // HD), axis=1),
        jnp.concatenate([-sine, sine] * (LANES // HD), axis=1),
    )


def project_kernel(x_ref, wq_ref, wk_ref, wv_ref, cos_ref, sin_ref, scale_ref, q0_ref, k0_ref, unit_ref):
    rows, per, _, length, width = unit_ref.shape
    block = wq_ref.shape[1]
    x = x_ref[...]
    q0 = matmul(x, wq_ref[...])
    k0 = matmul(x, wk_ref[...])
    v = matmul(x, wv_ref[...]).astype(BF)
    q0_ref[...] = q0
    k0_ref[...] = k0
    lanes = lane_ids(length)
    ones = head_blocks()
    per_tile = LANES // width
    for row in range(rows):
        for tile in range(block // LANES):
            there = (slice(row * length, (row + 1) * length), slice(tile * LANES, (tile + 1) * LANES))
            scale = scale_ref[:, tile * LANES : (tile + 1) * LANES]
            cosine = cos_ref[there[0], :]
            sine = sin_ref[there[0], :]
            results = []
            for raw in (q0, k0):
                z = raw[there]
                rot = z * cosine + swapped_halves(z, lanes) * sine
                total = split_dot(z * z, ones)
                results.append((rot * lax.rsqrt(total + 1e-06) * scale).astype(BF))
            results.append(v[there])
            for part in range(per_tile):
                for kind in range(3):
                    unit_ref[row, tile * per_tile + part, kind] = results[kind][
                        :, part * width : (part + 1) * width
                    ]


def project(x, wq, wk, wv, cosine, sine, scale, rows, width):
    tokens, model = x.shape
    length = tokens // rows
    block = 256
    per = block // width
    return pl.pallas_call(
        project_kernel,
        grid=(model // block,),
        in_specs=[
            pl.BlockSpec((tokens, model), lambda j: (0, 0)),
            pl.BlockSpec((model, block), lambda j: (0, j)),
            pl.BlockSpec((model, block), lambda j: (0, j)),
            pl.BlockSpec((model, block), lambda j: (0, j)),
            pl.BlockSpec((tokens, LANES), lambda j: (0, 0)),
            pl.BlockSpec((tokens, LANES), lambda j: (0, 0)),
            pl.BlockSpec((1, block), lambda j: (0, j)),
        ],
        out_specs=[
            pl.BlockSpec((tokens, block), lambda j: (0, j)),
            pl.BlockSpec((tokens, block), lambda j: (0, j)),
            pl.BlockSpec((rows, per, 3, length, width), lambda j: (0, j, 0, 0, 0)),
        ],
        out_shape=[
            jax.ShapeDtypeStruct((tokens, model), F32),
            jax.ShapeDtypeStruct((tokens, model), F32),
            jax.ShapeDtypeStruct((rows, model // width, 3, length, width), BF),
        ],
        name="project",
    )(x, wq, wk, wv, cosine, sine, scale)


def unproject_kernel(grad_ref, q0_ref, k0_ref, cos_ref, sin_ref, scale_ref, low_ref, gs_ref):
    rows, per, _, length, width = grad_ref.shape
    block = q0_ref.shape[1]
    model = low_ref.shape[1] // 3
    offset = pl.program_id(0) * block
    lanes = lane_ids(length)
    ones = head_blocks()
    per_tile = LANES // width
    for tile in range(block // LANES):
        across = slice(tile * LANES, (tile + 1) * LANES)
        scale = scale_ref[:, across]
        slope = jnp.zeros((1, LANES), F32)
        for row in range(rows):
            there = (slice(row * length, (row + 1) * length), across)
            cosine = cos_ref[there[0], :]
            sine = sin_ref[there[0], :]
            parts = []
            for kind in range(3):
                pieces = [grad_ref[row, tile * per_tile + part, kind] for part in range(per_tile)]
                parts.append(pieces[0] if per_tile == 1 else jnp.concatenate(pieces, axis=1))
            for kind, raw_ref in enumerate((q0_ref, k0_ref)):
                grad = parts[kind]
                z = raw_ref[there]
                g = grad.astype(F32)
                rot = z * cosine + swapped_halves(z, lanes) * sine
                inverse = lax.rsqrt(split_dot(z * z, ones) + 1e-06)
                unit = rot * inverse
                slope = slope + jnp.sum(g * unit, axis=0, keepdims=True)
                g = g * scale
                g = inverse * (g - unit * split_dot(g * unit, ones))
                g = g * cosine - swapped_halves(g, lanes) * sine
                parts[kind] = g.astype(BF)
            for kind in range(3):
                column = pl.multiple_of(kind * model + offset + tile * LANES, LANES)
                low_ref[there[0], pl.ds(column, LANES)] = parts[kind]
        gs_ref[:, across] = slope


def unproject(grad, q0, k0, cosine, sine, scale):
    rows, heads, _, length, width = grad.shape
    tokens, model = q0.shape
    block = 256
    per = block // width
    wide = pl.BlockSpec((tokens, block), lambda j: (0, j))
    table = pl.BlockSpec((tokens, LANES), lambda j: (0, 0))
    line = pl.BlockSpec((1, block), lambda j: (0, j))
    return pl.pallas_call(
        unproject_kernel,
        grid=(model // block,),
        in_specs=[
            pl.BlockSpec((rows, per, 3, length, width), lambda j: (0, j, 0, 0, 0)),
            wide,
            wide,
            table,
            table,
            line,
        ],
        out_specs=[pl.BlockSpec((tokens, 3 * model), lambda j: (0, 0)), line],
        out_shape=[
            jax.ShapeDtypeStruct((tokens, 3 * model), BF),
            jax.ShapeDtypeStruct((1, model), F32),
        ],
        name="unproject",
    )(grad, q0, k0, cosine, sine, scale)


def widened(values):
    rows, width = values.shape
    if width == LANES:
        return values
    return jnp.concatenate([values, jnp.zeros((rows, LANES - width), values.dtype)], axis=1)


def in_head(rows, head):
    return lane_ids(rows) // HD == head


def attend_kernel(low_ref, begin_ref, unit_ref, o_ref, inv_ref, qs, ks, vs, acc):
    sources, _, _, length, width = unit_ref.shape
    heads = width // HD
    block = acc.shape[1]
    count = sources * length // block
    unit = pl.program_id(0)
    chunk = block // length

    def prepare(source, carry):
        at = pl.ds(pl.multiple_of(source * length, length), length)
        q = widened(unit_ref[source, 0, 0]) * jnp.asarray(math.sqrt(HD), BF)
        v = widened(unit_ref[source, 0, 2])
        ks[at, :] = widened(unit_ref[source, 0, 1])
        for head in range(heads):
            own = in_head(length, head)
            qs[head, at, :] = jnp.where(own, q, jnp.zeros_like(q))
            vs[head, at, :] = jnp.where(own, v, jnp.ones_like(v))
        return carry

    lax.fori_loop(0, sources, prepare, 0)

    def query_turn(turn, carry):
        first = pl.multiple_of(turn * block, block)
        begin = jnp.broadcast_to(begin_ref[0, :, pl.ds(first, block)], (LANES, block))
        begin = jnp.transpose(begin)[:, :1]
        places = first + lax.broadcasted_iota(jnp.int32, (block, 1), 0)
        acc[...] = jnp.zeros_like(acc)

        def key_turn(other, inner):
            start = pl.multiple_of(other * block, block)
            keys = ks[pl.ds(start, block), :]
            across = start + lax.broadcasted_iota(jnp.int32, (1, block), 1)
            allowed = (across.astype(F32) >= begin) & (across <= places)
            for head in range(heads):
                scores = right_trans(qs[head, pl.ds(first, block), :], keys)
                expo = jnp.where(allowed, jnp.exp(scores), 0.0)
                acc[head] += matmul(expo.astype(BF), vs[head, pl.ds(start, block), :])
            return inner

        lax.fori_loop(low_ref[unit, turn], turn + 1, key_turn, 0)
        output = None
        inverse = None
        for head in range(heads):
            summed = acc[head]
            one = 1.0 / pltpu.roll(summed, HD, 1)
            two = summed * one
            if output is None:
                output, inverse = two, one
            else:
                own = in_head(block, head)
                output = jnp.where(own, two, output)
                inverse = jnp.where(own, one, inverse)
        for part in range(chunk):
            source = turn * chunk + part
            rows = slice(part * length, (part + 1) * length)
            o_ref[source, 0] = output[rows, :width].astype(BF)
            inv_ref[source, 0] = inverse[rows]
        return carry

    lax.fori_loop(0, count, query_turn, 0)


def attend(low, begin, unit, block):
    sources, units, _, length, width = unit.shape
    total = sources * length
    heads = width // HD
    return pl.pallas_call(
        attend_kernel,
        grid_spec=pltpu.PrefetchScalarGridSpec(
            num_scalar_prefetch=1,
            grid=(units,),
            in_specs=[
                pl.BlockSpec((1, 1, total), lambda u, low: (u, 0, 0)),
                pl.BlockSpec((sources, 1, 3, length, width), lambda u, low: (0, u, 0, 0, 0)),
            ],
            out_specs=[
                pl.BlockSpec((sources, 1, length, width), lambda u, low: (0, u, 0, 0)),
                pl.BlockSpec((sources, 1, length, LANES), lambda u, low: (0, u, 0, 0)),
            ],
            scratch_shapes=[
                pltpu.VMEM((heads, total, LANES), BF),
                pltpu.VMEM((total, LANES), BF),
                pltpu.VMEM((heads, total, LANES), BF),
                pltpu.VMEM((heads, block, LANES), F32),
            ],
        ),
        out_shape=[
            jax.ShapeDtypeStruct((sources, units, length, width), BF),
            jax.ShapeDtypeStruct((sources, units, length, LANES), F32),
        ],
        name="attend",
    )(low, begin, unit)


def attend_back_kernel(
    high_ref, begin_ref, unit_ref, go_ref, o_ref, inv_ref, grad_ref, qs, k8, ks, vs, da, dam, dq, dk, dv
):
    sources, _, _, length, width = unit_ref.shape
    heads = width // HD
    block = dk.shape[0]
    count = sources * length // block
    unit = pl.program_id(0)
    chunk = block // length
    root = jnp.asarray(math.sqrt(HD), BF)

    def prepare(source, carry):
        at = pl.ds(pl.multiple_of(source * length, length), length)
        q = widened(unit_ref[source, 0, 0]) * root
        k = widened(unit_ref[source, 0, 1])
        v = widened(unit_ref[source, 0, 2])
        ks[at, :] = k
        k = k * root
        go = widened(go_ref[source, 0]).astype(F32) * inv_ref[source, 0]
        product = go * widened(o_ref[source, 0]).astype(F32)
        for head in range(heads):
            own = in_head(length, head)
            qs[head, at, :] = jnp.where(own, q, jnp.zeros_like(q))
            k8[head, at, :] = jnp.where(own, k, jnp.zeros_like(k))
            vs[head, at, :] = jnp.where(own, v, jnp.ones_like(v))
            mine = jnp.where(own, go, 0.0)
            dam[head, at, :] = mine.astype(BF)
            slope = -jnp.sum(jnp.where(own, product, 0.0), axis=1, keepdims=True)
            spare = lane_ids(length) == ((head + 1) * HD) % LANES
            da[head, at, :] = jnp.where(spare, slope, mine).astype(BF)
        dq[at, :] = jnp.zeros((length, LANES), F32)
        return carry

    lax.fori_loop(0, sources, prepare, 0)

    def key_turn(turn, carry):
        start = pl.multiple_of(turn * block, block)
        keys = ks[pl.ds(start, block), :]
        along = start + lax.broadcasted_iota(jnp.int32, (block, 1), 0)
        dk[...] = jnp.zeros_like(dk)
        dv[...] = jnp.zeros_like(dv)

        def query_turn(other, inner):
            first = pl.multiple_of(other * block, block)
            begin = begin_ref[0, :, pl.ds(first, block)]
            across = first + lax.broadcasted_iota(jnp.int32, (1, block), 1)
            allowed = (along.astype(F32) >= begin) & (along <= across)
            for head in range(heads):
                queries = qs[head, pl.ds(first, block), :]
                scores = right_trans(keys, queries)
                expo = jnp.where(allowed, jnp.exp(scores), 0.0)
                slopes = right_trans(vs[head, pl.ds(start, block), :], da[head, pl.ds(first, block), :])
                slopes = (expo * slopes).astype(BF)
                dk[...] += matmul(slopes, queries)
                dv[...] += matmul(expo.astype(BF), dam[head, pl.ds(first, block), :])
                dq[pl.ds(first, block), :] += left_trans(slopes, k8[head, pl.ds(start, block), :])
            return inner

        lax.fori_loop(turn, high_ref[unit, turn] + 1, query_turn, 0)
        for part in range(chunk):
            source = turn * chunk + part
            rows = slice(part * length, (part + 1) * length)
            grad_ref[source, 0, 1] = dk[rows, :width].astype(BF)
            grad_ref[source, 0, 2] = dv[rows, :width].astype(BF)
        return carry

    lax.fori_loop(0, count, key_turn, 0)

    def finish(source, carry):
        at = pl.ds(pl.multiple_of(source * length, length), length)
        grad_ref[source, 0, 0] = dq[at, :width].astype(BF)
        return carry

    lax.fori_loop(0, sources, finish, 0)


def attend_back(high, begin, unit, go, o, inverse, block):
    sources, units, _, length, width = unit.shape
    total = sources * length
    heads = width // HD
    flat = pl.BlockSpec((sources, 1, length, width), lambda u, high: (0, u, 0, 0))
    triple = pl.BlockSpec((sources, 1, 3, length, width), lambda u, high: (0, u, 0, 0, 0))
    return pl.pallas_call(
        attend_back_kernel,
        grid_spec=pltpu.PrefetchScalarGridSpec(
            num_scalar_prefetch=1,
            grid=(units,),
            in_specs=[
                pl.BlockSpec((1, 1, total), lambda u, high: (u, 0, 0)),
                triple,
                flat,
                flat,
                pl.BlockSpec((sources, 1, length, LANES), lambda u, high: (0, u, 0, 0)),
            ],
            out_specs=[triple],
            scratch_shapes=[
                pltpu.VMEM((heads, total, LANES), BF),
                pltpu.VMEM((heads, total, LANES), BF),
                pltpu.VMEM((total, LANES), BF),
                pltpu.VMEM((heads, total, LANES), BF),
                pltpu.VMEM((heads, total, LANES), BF),
                pltpu.VMEM((heads, total, LANES), BF),
                pltpu.VMEM((total, LANES), F32),
                pltpu.VMEM((block, LANES), F32),
                pltpu.VMEM((block, LANES), F32),
            ],
        ),
        out_shape=[jax.ShapeDtypeStruct((sources, units, 3, length, width), BF)],
        name="attend_back",
    )(high, begin, unit, go, o, inverse)[0]


def unit_scale(values):
    return lax.rsqrt(jnp.mean(values * values, axis=-1, keepdims=True) + 1e-06)


def blend_forward(hidden, branch, alpha):
    scale = unit_scale(branch)
    normal = branch * scale
    mixture = hidden + alpha * (normal - hidden)
    outer = unit_scale(mixture)
    return scale, normal, outer, mixture * outer


def blend_backward(grad, hidden, alpha, scale, normal, outer, result):
    inside = outer * (grad - result * jnp.mean(grad * result, axis=-1, keepdims=True))
    slope = jnp.sum(inside * (normal - hidden), axis=0, keepdims=True)
    on_normal = alpha * inside
    on_branch = scale * (on_normal - normal * jnp.mean(on_normal * normal, axis=-1, keepdims=True))
    return inside - on_normal, on_branch, slope


def feed_kernel(
    unit_ref, x_ref, cot_ref, wo_ref, wu_ref, wg_ref, wd_ref, aa_ref, af_ref, us_ref, gs_ref,
    y_ref, mixed_ref, attn_ref, low_ref, up_ref, gate_ref, inner_ref, branch_ref, grad_ref, slope_ref,
    middle, total,
):
    rows, groups, length, width = unit_ref.shape
    turn = pl.program_id(0)

    @pl.when(turn == 0)
    def _():
        per_tile = LANES // width
        for row in range(rows):
            for tile in range(groups // per_tile):
                pieces = [unit_ref[row, tile * per_tile + part] for part in range(per_tile)]
                piece = pieces[0] if per_tile == 1 else jnp.concatenate(pieces, axis=1)
                mixed_ref[row * length : (row + 1) * length, tile * LANES : (tile + 1) * LANES] = piece
        attn = matmul(mixed_ref[...], wo_ref[...])
        attn_ref[...] = attn
        _, _, _, result = blend_forward(x_ref[...].astype(F32), attn, aa_ref[...])
        middle[...] = result
        low_ref[...] = result.astype(BF)
        total[...] = jnp.zeros_like(total)

    low = low_ref[...]
    up = matmul(low, wu_ref[...])
    gate = matmul(low, wg_ref[...])
    up_ref[...] = up
    gate_ref[...] = gate
    z = gate * gs_ref[...]
    inner = (up * us_ref[...] * (z / (1.0 + jnp.exp(-z)))).astype(BF)
    inner_ref[...] = inner
    total[...] += matmul(inner, wd_ref[...])

    @pl.when(turn == pl.num_programs(0) - 1)
    def _():
        hidden = middle[...]
        alpha = af_ref[...]
        scale, normal, outer, result = blend_forward(hidden, total[...], alpha)
        y_ref[...] = result.astype(BF)
        on_hidden, on_branch, slope = blend_backward(
            cot_ref[...].astype(F32), hidden, alpha, scale, normal, outer, result
        )
        grad_ref[...] = on_hidden
        branch_ref[...] = on_branch.astype(BF)
        slope_ref[...] = slope


def feed(unit, x, cot, wo, wu, wg, wd, aa, af, us, gs):
    tokens, model = x.shape
    deep = wu.shape[1]
    tile = 512
    whole = pl.BlockSpec((tokens, model), lambda j: (0, 0))
    across = pl.BlockSpec((tokens, tile), lambda j: (0, j))
    line = pl.BlockSpec((1, model), lambda j: (0, 0))
    cut = pl.BlockSpec((1, tile), lambda j: (0, j))
    side = pl.BlockSpec((model, tile), lambda j: (0, j))
    act = lambda kind, size: jax.ShapeDtypeStruct((tokens, size), kind)
    return pl.pallas_call(
        feed_kernel,
        grid=(deep // tile,),
        in_specs=[
            pl.BlockSpec(unit.shape, lambda j: (0, 0, 0, 0)),
            whole,
            whole,
            pl.BlockSpec((model, model), lambda j: (0, 0)),
            side,
            side,
            pl.BlockSpec((tile, model), lambda j: (j, 0)),
            line,
            line,
            cut,
            cut,
        ],
        out_specs=[whole, whole, whole, whole, across, across, across, whole, whole, line],
        out_shape=[
            act(BF, model),
            act(BF, model),
            act(F32, model),
            act(BF, model),
            act(F32, deep),
            act(F32, deep),
            act(BF, deep),
            act(BF, model),
            act(F32, model),
            jax.ShapeDtypeStruct((1, model), F32),
        ],
        scratch_shapes=[pltpu.VMEM((tokens, model), F32), pltpu.VMEM((tokens, model), F32)],
        name="feed",
    )(unit, x, cot, wo, wu, wg, wd, aa, af, us, gs)


def feed_back_kernel(
    branch_ref, up_ref, gate_ref, grad_ref, x_ref, attn_ref, wo_ref, wu_ref, wg_ref, wd_ref, aa_ref, us_ref, gs_ref,
    pair_ref, attended_ref, hidden_ref, unit_ref, us_slope, gs_slope, aa_slope,
    total,
):
    rows, groups, length, width = unit_ref.shape
    turn = pl.program_id(0)

    @pl.when(turn == 0)
    def _():
        total[...] = grad_ref[...]

    grad = right_trans(branch_ref[...], wd_ref[...])
    up = up_ref[...]
    gate = gate_ref[...]
    scale = us_ref[...]
    z = gate * gs_ref[...]
    soft = 1.0 / (1.0 + jnp.exp(-z))
    silu = z * soft
    along = grad * silu
    us_slope[...] = jnp.sum(along * up, axis=0, keepdims=True)
    up_low = (along * scale).astype(BF)
    inside = grad * up * scale * (soft * (1.0 + z * (1.0 - soft)))
    gs_slope[...] = jnp.sum(inside * gate, axis=0, keepdims=True)
    gate_low = (inside * gs_ref[...]).astype(BF)
    pair_ref[0] = up_low
    pair_ref[1] = gate_low
    total[...] += right_trans(up_low, wu_ref[...]) + right_trans(gate_low, wg_ref[...])

    @pl.when(turn == pl.num_programs(0) - 1)
    def _():
        hidden = x_ref[...].astype(F32)
        alpha = aa_ref[...]
        scale, normal, outer, result = blend_forward(hidden, attn_ref[...], alpha)
        on_hidden, on_branch, slope = blend_backward(total[...], hidden, alpha, scale, normal, outer, result)
        hidden_ref[...] = on_hidden
        low = on_branch.astype(BF)
        attended_ref[...] = low
        aa_slope[...] = slope
        back = right_trans(low, wo_ref[...]).astype(BF)
        for row in range(rows):
            for group in range(groups):
                unit_ref[row, group] = back[
                    row * length : (row + 1) * length, group * width : (group + 1) * width
                ]


def feed_back(branch, up, gate, grad, x, attn, wo, wu, wg, wd, aa, us, gs, rows, width):
    tokens, model = x.shape
    deep = wu.shape[1]
    tile = 512
    whole = pl.BlockSpec((tokens, model), lambda j: (0, 0))
    across = pl.BlockSpec((tokens, tile), lambda j: (0, j))
    line = pl.BlockSpec((1, model), lambda j: (0, 0))
    cut = pl.BlockSpec((1, tile), lambda j: (0, j))
    side = pl.BlockSpec((model, tile), lambda j: (0, j))
    unit_shape = (rows, model // width, tokens // rows, width)
    return pl.pallas_call(
        feed_back_kernel,
        grid=(deep // tile,),
        in_specs=[
            whole,
            across,
            across,
            whole,
            whole,
            whole,
            pl.BlockSpec((model, model), lambda j: (0, 0)),
            side,
            side,
            pl.BlockSpec((tile, model), lambda j: (j, 0)),
            line,
            cut,
            cut,
        ],
        out_specs=[
            pl.BlockSpec((2, tokens, tile), lambda j: (0, 0, j)),
            whole,
            whole,
            pl.BlockSpec(unit_shape, lambda j: (0, 0, 0, 0)),
            cut,
            cut,
            line,
        ],
        out_shape=[
            jax.ShapeDtypeStruct((2, tokens, deep), BF),
            jax.ShapeDtypeStruct((tokens, model), BF),
            jax.ShapeDtypeStruct((tokens, model), F32),
            jax.ShapeDtypeStruct(unit_shape, BF),
            jax.ShapeDtypeStruct((1, deep), F32),
            jax.ShapeDtypeStruct((1, deep), F32),
            jax.ShapeDtypeStruct((1, model), F32),
        ],
        scratch_shapes=[pltpu.VMEM((tokens, model), F32)],
        name="feed_back",
    )(branch, up, gate, grad, x, attn, wo, wu, wg, wd, aa, us, gs)


def position_of(relative, order):
    bits = len(order)
    return sum(((relative >> bit) & 1) << (bits - 1 - place) for place, bit in enumerate(order))


def weight_kernel(where_ref, *refs, segments, chains, count):
    ins = refs[: 4 * len(segments)]
    outs = refs[4 * len(segments) : -2]
    turned, right = refs[-2:]
    deep = turned.shape[0]
    tokens = turned.shape[1] // 2
    height = deep // count
    turn = pl.program_id(0)
    me = where_ref[0]
    first = 0
    for index, tiles in enumerate(segments):
        own_left, pair_left, own_right, pair_right = ins[4 * index : 4 * index + 4]

        @pl.when(turn == first)
        def _():
            for side, left in enumerate((own_left, pair_left)):
                flipped = jnp.transpose(left[...])
                for source in range(count):
                    target = pl.multiple_of((me ^ source) * height, height)
                    turned[pl.ds(target, height), side * tokens : (side + 1) * tokens] = flipped[
                        source * height : (source + 1) * height
                    ]

        @pl.when((turn >= first) & (turn < first + tiles))
        def _():
            right[:tokens] = own_right[...].reshape(right[:tokens].shape)
            right[tokens:] = pair_right[...]

        first += tiles
    chunk = max(height, min(deep, 512))
    first = 0
    for index, (tiles, order) in enumerate(chains):
        send_ref, keep_ref = outs[2 * index : 2 * index + 2]

        @pl.when((turn >= first) & (turn < first + tiles))
        def _():
            for start in range(0, deep, chunk):
                block = matmul(turned[start : start + chunk], right[...]).astype(BF)
                for inside in range(chunk // height):
                    place = position_of(start // height + inside, order)
                    piece = block[inside * height : (inside + 1) * height]
                    if place >= count // 2:
                        send_ref[place - count // 2] = piece
                    else:
                        keep_ref[place] = piece

        first += tiles


def weight_terms(place, seqs, segments, chains, tile):
    tokens, deep = segments[0][0].shape
    height = deep // seqs
    in_specs = []
    operands = []
    tiles_of = []
    first = 0
    for own_left, pair_left, own_right, pair_right in segments:
        tiles = pair_right.shape[1] // tile
        tiles_of.append(tiles)
        held = pl.BlockSpec((tokens, deep), lambda j, where: (0, 0))
        inside = lambda j, first=first, tiles=tiles: jnp.clip(j - first, 0, tiles - 1)
        if own_right.ndim == 3:
            own = pl.BlockSpec((1, tokens, tile), lambda j, where, inside=inside: (where[1], 0, inside(j)))
        else:
            own = pl.BlockSpec(
                (tokens, tile), lambda j, where, inside=inside, tiles=tiles: (0, where[1] * tiles + inside(j))
            )
        pair = pl.BlockSpec((tokens, tile), lambda j, where, inside=inside: (0, inside(j)))
        in_specs += [held, held, own, pair]
        operands += [own_left, pair_left, own_right, pair_right]
        first += tiles
    out_specs = []
    out_shape = []
    start = 0
    for tiles, _ in chains:
        spec = pl.BlockSpec(
            (seqs // 2, height, tile),
            lambda j, where, start=start, tiles=tiles: (0, 0, jnp.clip(j - start, 0, tiles - 1)),
        )
        out_specs += [spec, spec]
        out_shape += [jax.ShapeDtypeStruct((seqs // 2, height, tiles * tile), BF)] * 2
        start += tiles
    assert start == first
    kernel = lambda *refs: weight_kernel(*refs, segments=tuple(tiles_of), chains=chains, count=seqs)
    outs = pl.pallas_call(
        kernel,
        grid_spec=pltpu.PrefetchScalarGridSpec(
            num_scalar_prefetch=1,
            grid=(first,),
            in_specs=in_specs,
            out_specs=out_specs,
            scratch_shapes=[pltpu.VMEM((deep, 2 * tokens), BF), pltpu.VMEM((2 * tokens, tile), BF)],
        ),
        out_shape=out_shape,
        name="weight_terms",
    )(place, *operands)
    return [(outs[2 * i], outs[2 * i + 1], order) for i, (_, order) in enumerate(chains)]


def after(values, other):
    return lax.optimization_barrier((values, other))[0]


class Reduction:
    def __init__(self, terms, name):
        self.terms = terms
        self.name = name
        self.got = [[] for _ in terms]
        self.step = 0
        self.moving = [send for send, _, _ in terms]

    def start(self):
        for index, (_, _, order) in enumerate(self.terms):
            bit = order[self.step]
            count = 1 << len(order)
            with jax.named_scope(f"{self.name}_{index}_{self.step}"):
                taken = lax.ppermute(self.moving[index], "seq", [(i, i ^ (1 << bit)) for i in range(count)])
            self.got[index].append(taken)
        self.step += 1
        return self

    def hold(self, other):
        for got in self.got:
            got[-1] = after(got[-1], other)
        return self

    def add(self):
        for index, (_, keep, order) in enumerate(self.terms):
            size = (1 << len(order)) >> (self.step + 1)
            part = slice(size, 2 * size) if size else slice(0, 1)
            moving = keep[part].astype(F32)
            for piece in self.got[index]:
                moving = moving + piece[part].astype(F32)
            self.moving[index] = moving.astype(BF) if size else moving[0]
        return self

    def result(self):
        return self.moving[0] if len(self.moving) == 1 else jnp.concatenate(self.moving, axis=1)


def paired(values):
    count = lax.axis_size("batch")
    return lax.ppermute(values, "batch", [(i, i ^ 1) for i in range(count)])


def batch_finished(values):
    count = lax.axis_size("batch")
    mine = lax.axis_index("batch")
    height, half_width = values.shape
    values = values.reshape(count, height // count, half_width)
    bit = count.bit_length() - 2
    while bit > 0:
        values = values.reshape((2, values.shape[0] // 2) + values.shape[1:])
        side = (mine >> bit) & 1
        sent = lax.dynamic_index_in_dim(values, 1 - side, 0, keepdims=False)
        kept = lax.dynamic_index_in_dim(values, side, 0, keepdims=False)
        pairs = [(i, i ^ (1 << bit)) for i in range(count)]
        values = kept + lax.ppermute(sent, "batch", pairs)
        bit -= 1
    side = mine & 1
    sent = lax.dynamic_index_in_dim(values, 1 - side, 0, keepdims=False)
    kept = lax.dynamic_index_in_dim(values, side, 0, keepdims=False)
    taken = paired(sent)
    first = jnp.where(side == 0, kept, taken)
    second = jnp.where(side == 0, taken, kept)
    return first, second


def joined(halves):
    return jnp.concatenate(halves, axis=1)


def other_half(values):
    side = lax.axis_index("batch") & 1
    half = values.shape[1] // 2
    return paired(lax.dynamic_slice_in_dim(values, (1 - side) * half, half, 1))


def body(
    hidden_in,
    segment_ids,
    query_weight,
    key_weight,
    value_weight,
    out_weight,
    up_weight,
    gate_weight,
    down_weight,
    alpha_attend,
    alpha_feed,
    score_scale,
    up_scale,
    gate_scale,
    cotangent,
):
    rows, length, width = hidden_in.shape
    tokens = rows * length
    seqs = lax.axis_size("seq")
    batches = lax.axis_size("batch")
    me = lax.axis_index("seq")
    side = lax.axis_index("batch") & 1
    place = jnp.stack([me, side]).astype(jnp.int32)
    total = seqs * length
    pack = LANES // HD
    if (H // pack * rows) % seqs:
        pack = 1
    span = pack * HD
    groups = H // pack
    units = groups * rows // seqs
    block = math.gcd(256, total)
    bits = tuple(range(seqs.bit_length() - 1))
    order_a = bits
    order_b = bits[1:3] + bits[:1] + bits[3:]
    order_c = bits[2:3] + bits[:2] + bits[3:]
    order_d = (1, 0) + bits[2:]

    def exchanged(values, name):
        with jax.named_scope(name):
            return lax.all_to_all(values, "seq", 0, 0, tiled=True)

    ids = exchanged(jnp.broadcast_to(segment_ids[None], (seqs, rows, length)), "swap_ids")
    ids = jnp.transpose(ids.reshape(seqs, rows, length), (1, 0, 2)).reshape(rows, total)
    labels = jnp.arange(SEGS, dtype=jnp.int32)
    starts = jnp.sum(ids[:, None, :] < labels[None, :, None], axis=2)
    places = me * length + jnp.arange(length, dtype=jnp.int32)
    match = segment_ids[:, None, :] == labels[None, :, None]
    offsets = places[None, :] - jnp.sum(jnp.where(match, starts[:, :, None], 0), axis=1)
    cosine, sine = rope_tables(offsets.reshape(tokens))
    unit_rows = (me * units + jnp.arange(units, dtype=jnp.int32)) // groups
    ids = jnp.take(ids, unit_rows, axis=0)
    starts = jnp.sum(ids[:, None, :] < labels[None, :, None], axis=2)
    ends = jnp.sum(ids[:, None, :] <= labels[None, :, None], axis=2)
    match = ids[:, None, :] == labels[None, :, None]
    begin = jnp.sum(jnp.where(match, starts[:, :, None], 0), axis=1)
    end = jnp.sum(jnp.where(match, ends[:, :, None], 0), axis=1)
    low = (begin[:, ::block] // block).astype(jnp.int32)
    high = ((end[:, block - 1 :: block] - 1) // block).astype(jnp.int32)
    begin = begin.astype(F32).reshape(units, 1, total)

    flat_in = hidden_in.reshape(tokens, width)
    flat_cot = cotangent.reshape(tokens, width)
    scale_row = score_scale.reshape(1, width)
    alpha_one = alpha_attend.reshape(1, width)
    alpha_two = alpha_feed.reshape(1, width)
    up_row = up_scale.reshape(1, -1)
    gate_row = gate_scale.reshape(1, -1)

    query_raw, key_raw, sent = project(
        flat_in, query_weight, key_weight, value_weight, cosine, sine, scale_row, rows, span
    )
    unit = exchanged(sent.reshape(rows * groups, 3, length, span), "swap_qkv")
    unit = unit.reshape(seqs, units, 3, length, span)
    out_unit, inverse = attend(low, begin, unit, block)
    mixed_unit = exchanged(out_unit.reshape(seqs * units, length, span), "swap_o")
    mixed_unit = mixed_unit.reshape(rows, groups, length, span)

    (layer_out, mixed, attended, middle_low, up_part, gate_part, inner_low, branch_low, middle_grad, feed_slope) = feed(
        mixed_unit, flat_in, flat_cot, out_weight, up_weight, gate_weight, down_weight,
        alpha_one, alpha_two, up_row, gate_row,
    )
    pair_inner = paired(inner_low)
    pair_branch = other_half(branch_low)
    (stacked, attended_low, hidden_grad, go_sent, up_slope, gate_slope, attend_slope) = feed_back(
        branch_low, up_part, gate_part, middle_grad, flat_in, attended, out_weight, up_weight, gate_weight,
        down_weight, alpha_one, up_row, gate_row, rows, span,
    )
    go_unit = exchanged(go_sent.reshape(rows * groups, length, span), "swap_go").reshape(seqs, units, length, span)

    pair_middle = paired(middle_low)
    pair_mixed = paired(mixed)
    pair_in = paired(flat_in)
    pair_stacked = paired(lax.dynamic_index_in_dim(stacked, 1 - side, 0, keepdims=False))
    pair_attended = other_half(attended_low)

    down = Reduction(
        weight_terms(
            after(place, go_sent),
            seqs,
            [(inner_low, pair_inner, branch_low, pair_branch)],
            ((1, order_a), (1, order_d)),
            256,
        ),
        "down",
    ).start()
    feeds = Reduction(
        weight_terms(
            after(place, down.moving[0]),
            seqs,
            [(middle_low, pair_middle, stacked, pair_stacked), (mixed, pair_mixed, attended_low, pair_attended)],
            ((6, order_a), (6, order_b), (6, order_c)),
            256,
        ),
        "feeds",
    )

    grad_unit = attend_back(high, begin, unit, go_unit, out_unit, inverse, block)
    grads = exchanged(grad_unit.reshape(seqs * units, 3, length, span), "swap_grads")
    grads = grads.reshape(rows, groups, 3, length, span)
    down.hold(grad_unit).add().start()
    feeds.moving = [after(moving, grad_unit) for moving in feeds.moving]
    feeds.start()
    for _ in bits[2:]:
        down.add().start()

    low_all, score_slope = unproject(grads, query_raw, key_raw, cosine, sine, scale_row)
    pair_low = other_half(low_all)
    qkv = Reduction(
        weight_terms(
            place, seqs, [(flat_in, pair_in, low_all, pair_low)], ((2, order_a), (2, order_b), (2, order_c)), 256
        ),
        "qkv",
    ).start()
    input_grad = (
        hidden_grad
        + right_trans(low_all[:, :width], query_weight)
        + right_trans(low_all[:, width : 2 * width], key_weight)
        + right_trans(low_all[:, 2 * width :], value_weight)
    )
    feeds.hold(qkv.moving[0])
    for _ in bits[1:]:
        feeds.add().start()
        qkv.add().start()
    down_gradient = joined(batch_finished(down.add().result()))
    feed_halves = batch_finished(feeds.add().result())
    wide = feed_halves[0].shape[1] - width // 2
    up_gradient = feed_halves[0][:, :wide]
    gate_gradient = feed_halves[1][:, :wide]
    out_gradient = joined([half[:, wide:] for half in feed_halves])
    qkv_gradient = joined(batch_finished(qkv.add().result()))
    query_gradient, key_gradient, value_gradient = jnp.split(qkv_gradient, 3, axis=1)

    def summed(parts):
        devices = seqs * batches
        cuts = [part.reshape(devices, part.size // devices) for part in parts]
        mine = lax.all_to_all(jnp.concatenate(cuts, axis=1), ("seq", "batch"), 0, 0, tiled=True)
        mine = jnp.sum(mine, axis=0)
        outs = []
        at = 0
        for cut in cuts:
            outs.append(mine[at : at + cut.shape[1]])
            at += cut.shape[1]
        return outs

    small = summed((attend_slope, feed_slope, up_slope, gate_slope, score_slope))
    return (
        layer_out.reshape(rows, length, width),
        input_grad.reshape(rows, length, width),
        query_gradient,
        key_gradient,
        value_gradient,
        out_gradient,
        up_gradient,
        gate_gradient,
        down_gradient,
        small[0],
        small[1],
        small[4],
        small[2],
        small[3],
    )


def solution(mesh):
    wide = P("batch", "seq", None)
    in_specs = (wide, P("batch", "seq")) + (P(),) * 12 + (wide,)
    split = P(("seq", "batch"), None)
    out_specs = (wide, wide) + (split,) * 7 + (P(("seq", "batch")),) * 5
    return jax.shard_map(body, mesh=mesh, in_specs=in_specs, out_specs=out_specs, check_vma=False)
```
